32 devices in a mesh: groups: 2 (over x), req: 16 (over z, y, core).
Axes of the slice: x: 2, y: 2, z: 4, core: 2. Of those that a mesh axis runs over, the one named last changes fastest.
Arguments:
- queries: bfloat16 [2, 2048, 512], P(None, ('groups', 'req')), parts along dimension 1, may hold values from -40 to 40
- new_kv: bfloat16 [2, 2048, 128], P(None, ('groups', 'req')), parts along dimension 1, may hold values from -4 to 4
- cache: bfloat16 [2, 2048, 128, 128], P(None, ('groups', 'req')), parts along dimension 1, may hold values from -4 to 4
- lengths: int32 [2, 256], P(None, 'groups'), parts along dimension 1, may hold values from 2 to 128
- residual: bfloat16 [2, 256, 2880], P(None, ('groups', 'req')), parts along dimension 1, may hold values from -30 to 30
- o_proj: bfloat16 [4096, 2880], P('req'), may hold values from -1 to 1
- router: bfloat16 [2880, 16], replicated, may hold values from -0.109375 to 0.109375
- w_gate: bfloat16 [64, 2880, 360], P('req'), may hold values from -0.109375 to 0.109375
- w_up: bfloat16 [64, 2880, 360], P('req'), may hold values from -0.109375 to 0.109375
- w_down: bfloat16 [64, 360, 2880], P('req'), may hold values from -0.15625 to 0.15625
- routes: int32 [2, 256, 4], P(None, ('groups', 'req')), parts along dimension 1, may hold values from 0 to 15, all different within a row; in each aligned block of 8 rows (0 to 7, 8 to 15, ..., all dimensions but the last counted through in order) at most 4 rows name the same one
Outputs:
- attended: bfloat16 [2, 256, 2880], P(None, ('groups', 'req')), parts along dimension 1
- layer_out: bfloat16 [2, 256, 2880], P(None, ('groups', 'req')), parts along dimension 1
The draws below stay inside these ranges and needn't reach their ends.
There are 2 independent parts, one for each index of `groups`. The reference program is written for one: setup_inputs(seed, part) draws one part's arguments, and reference() takes and returns one part's arrays. A program takes and returns all parts, laid end to end along the dimension named above; an argument that names none is the same for every part. Nothing has to cross between parts.
Inputs may be any that keep to these rules, and one draw needn't show every extreme that they name: `routes`: each row names 4 different experts; of the 8 rows of one device of one micro-batch at most 4 name any one expert, and in every draw some expert is named by exactly 4 rows of some device.
All inputs are finite; a program needn't handle non-finite values.
Results may differ from the reference program's by a relative error of at most 0.0075.
Values may be sent and summed in bfloat16 or wider, within the bound.
A program may use at most 128 MiB of HBM per device.

```python
import math
import jax
import jax.numpy as jnp
import numpy as np
from jax import lax

D = 2880
HD = 64
KVH = 8
QPK = 8
WIN = 128
EXPERTS = 16
FFW = 1440
SPLIT = 4
TOPK = 4
MB = 2
REQ_DEV = 8
FFS = 360
REQS = 128
CAP = 4


def draw_queries(key, part):
    shape_full = (MB, KVH * REQS, QPK * HD)
    values = jnp.clip(jax.random.normal(jax.random.fold_in(key, 1), shape_full, jnp.float32), -4.0, 4.0)
    return values.astype(jnp.bfloat16)


def draw_cache(key, part):
    shape_full = (MB, KVH * REQS, WIN, 2 * HD)
    values = jnp.clip(jax.random.normal(jax.random.fold_in(key, 2), shape_full, jnp.float32), -4.0, 4.0)
    return values.astype(jnp.bfloat16)


def draw_residual(key, part):
    shape_full = (MB, REQS, D)
    base = 0.5 * jnp.clip(jax.random.normal(jax.random.fold_in(key, 3), shape_full, jnp.float32), -3.0, 3.0)
    row_scale = jnp.exp(jax.random.uniform(jax.random.fold_in(key, 4), (MB, REQS, 1), jnp.float32, -1.15, 1.15))
    column_scale = jnp.exp(jax.random.uniform(jax.random.fold_in(key, 5), (1, 1, D), jnp.float32, -1.15, 1.15))
    return (base * row_scale * column_scale).astype(jnp.bfloat16)


def touch_ends(values, key, smallest, largest):
    place = [jax.random.randint(jax.random.fold_in(key, axis), (), 0, length) for axis, length in enumerate(values.shape)]
    main_axis = values.shape.index(max(values.shape))
    next_to = place[:main_axis] + [(place[main_axis] + 1) % values.shape[main_axis]] + place[main_axis + 1:]
    return values.at[tuple(place)].set(smallest).at[tuple(next_to)].set(largest)


def block_levels(rng, shape, pieces, low, largest):
    factor_of = 1.0
    for dim, shards_of in pieces:
        draws = jax.random.uniform(jax.random.fold_in(jax.random.fold_in(rng, 6), dim), (shards_of,), jnp.float32, low / len(pieces), largest / len(pieces))
        factor_of = factor_of * jnp.repeat(jnp.exp(draws), shape[dim] // shards_of).reshape((-1,) + (1,) * (len(shape) - 1 - dim))
    return factor_of


def deal_out(stream_key, own, number, rows, number_of, top, limit, skew):
    ranking = jax.random.permutation(stream_key, number_of)
    heavy_load, common = shares(number_of, rows * top, limit, skew, True), shares(number_of, rows * top, limit, skew, False)
    places = jnp.arange(number_of)

    def named(sizes, turn):
        used = int((sizes > 0).sum())
        fixed = max(1, used // 4)
        moved = fixed + (places - fixed + turn * (used - fixed)) % max(1, number_of - fixed)
        return jnp.zeros((number_of,), jnp.int32).at[ranking[jnp.where(places < fixed, places, moved)]].set(jnp.asarray(sizes, jnp.int32))

    sizes = jnp.where(number % 4 == 0, named(heavy_load, number // 4), named(common, number - number // 4 - 1))
    mixed = jax.random.permutation(jax.random.fold_in(own, 3), number_of)
    giver, receiver = mixed[0:number_of // 2 * 2:2], mixed[1:number_of // 2 * 2:2]
    slack = jnp.minimum(sizes[giver] - 1, limit - sizes[receiver]) // 2
    slack = jnp.where((giver == ranking[0]) | (receiver == ranking[0]) | (sizes[receiver] == 0), 0, jnp.maximum(slack, 0))
    moved = jax.random.randint(jax.random.fold_in(own, 4), (number_of // 2,), 0, 1 << 20) % (slack + 1)
    sizes = sizes.at[giver].add(-moved).at[receiver].add(moved)
    members = jnp.searchsorted(jnp.cumsum(sizes), jnp.arange(rows * top), side="right").astype(jnp.int32)
    grid = members.reshape(top, rows).T
    grid = grid[jax.random.permutation(jax.random.fold_in(own, 1), rows)]
    turn = jax.random.randint(jax.random.fold_in(own, 2), (rows, 1), 0, top)
    return jnp.take_along_axis(grid, (jnp.arange(top)[None, :] + turn) % top, axis=1)


def shares(number_of, total, most, lean, full):
    weights = [(1 << 20) // math.isqrt(grade ** lean) + 1 for grade in range(1, number_of + 1)]
    largest = most if full else min(most, max(-(-total // number_of), total * weights[0] // sum(weights)))
    least = 1 if total - largest >= number_of - 1 else 0
    given, spare = [largest] + [least] * (number_of - 1), total - largest - least * (number_of - 1)
    while spare > 0:
        movable = [i for i in range(1, number_of) if given[i] < largest] or [i for i in range(1, number_of) if given[i] < most]
        mass, remaining = sum([weights[i] for i in movable]), spare
        for i in movable:
            more = min(most - given[i], max(1, remaining * weights[i] // mass), spare)
            given[i] = given[i] + more
            spare = spare - more
    return np.array(given)


def bell_draw(own_key, dims, width, most, pieces=(), kind=jnp.bfloat16):
    values = jax.random.normal(own_key, dims, jnp.float32) * width
    if len(pieces) > 0:
        values = block_levels(own_key, dims, pieces, -0.22, 0.18) * values
    return jnp.clip(values, min=-most, max=most).astype(kind)


def setup_inputs(seed: int = 0, part: int = 0) -> dict:
    keys = jax.random.split(jax.random.key(seed), 12)
    part_splits = jax.random.split(jax.random.fold_in(keys[11], part), 12)
    queries = draw_queries(jax.random.fold_in(jax.random.fold_in(keys[11], part), 71), part)
    new_kv = bell_draw(part_splits[1], (MB, KVH * REQS, 2 * HD), 1.0, 4.0, ((1, 16),))
    cache = draw_cache(jax.random.fold_in(jax.random.fold_in(keys[11], part), 71), part)
    lengths = touch_ends(jax.random.randint(part_splits[3], (MB, REQS), 2, WIN + 1), jax.random.fold_in(part_splits[3], 1), 2, WIN).astype(jnp.int32)
    residual = draw_residual(jax.random.fold_in(jax.random.fold_in(keys[11], part), 71), part)
    o_proj = bell_draw(keys[5], (KVH * QPK * HD, D), 0.0625, 1.0, ((0, 16),))
    router = bell_draw(keys[6], (D, EXPERTS), D ** -0.5, 0.109375)
    w_gate = bell_draw(keys[7], (EXPERTS * SPLIT, D, FFS), D ** -0.5, 0.109375, ((0, 16),))
    w_up = bell_draw(keys[8], (EXPERTS * SPLIT, D, FFS), D ** -0.5, 0.109375, ((0, 16),))
    w_down = bell_draw(keys[9], (EXPERTS * SPLIT, FFS, D), FFW ** -0.5, 0.15625, ((0, 16),))
    routes_keys = jax.random.split(jax.random.fold_in(part_splits[10], 1), MB * REQS // REQ_DEV)
    routes_turns = jax.random.permutation(jax.random.fold_in(part_splits[10], 3), MB * REQS // REQ_DEV)
    routes = jax.vmap(lambda own, number: deal_out(jax.random.fold_in(part_splits[10], 2), own, number, REQ_DEV, EXPERTS, TOPK, CAP, 2))(routes_keys, routes_turns).reshape((MB, REQS, TOPK))
    return dict(queries=queries, new_kv=new_kv, cache=cache, lengths=lengths, residual=residual, o_proj=o_proj, router=router, w_gate=w_gate, w_up=w_up, w_down=w_down, routes=routes)


def attention_rows(query_rows, new_pair, cache_rows, live_count):
    row_total = query_rows.shape[0]
    query_heads = query_rows.reshape(row_total, QPK, HD).astype(jnp.float32)
    keys_cached = cache_rows[:, :, :HD].astype(jnp.float32)
    values_cached = cache_rows[:, :, HD:].astype(jnp.float32)
    key_fresh = new_pair[:, :HD].astype(jnp.float32)
    value_fresh = new_pair[:, HD:].astype(jnp.float32)
    factor = 1.0 / math.sqrt(HD)
    scores = jnp.einsum('rqd,rpd->rqp', query_heads, keys_cached) * factor
    own_score = jnp.einsum('rqd,rd->rq', query_heads, key_fresh) * factor
    live = jnp.arange(WIN)[None, None, :] < live_count[:, None, None]
    masked = jnp.where(live, scores, -jnp.inf)
    top_score = jnp.maximum(lax.optimization_barrier(jnp.max(masked, axis=2)), own_score)
    weight_cached = jnp.exp(masked - top_score[:, :, None])
    weight_own = jnp.exp(own_score - top_score)
    total = lax.optimization_barrier(jnp.sum(weight_cached, axis=2)) + weight_own
    prob_cached = lax.optimization_barrier((weight_cached / total[:, :, None]).astype(jnp.bfloat16))
    prob_own = lax.optimization_barrier((weight_own / total).astype(jnp.bfloat16))
    mixed = jnp.einsum('rqp,rpd->rqd', prob_cached.astype(jnp.float32), values_cached)
    mixed = mixed + prob_own.astype(jnp.float32)[:, :, None] * value_fresh[:, None, :]
    return mixed.astype(jnp.bfloat16).reshape(row_total, QPK * HD)

def expert_block(operands):
    rows_in, gate_full, up_full, down_full = operands
    gate_hidden = jnp.dot(rows_in, gate_full, preferred_element_type=jnp.float32)
    up_hidden = jnp.dot(rows_in, up_full, preferred_element_type=jnp.float32)
    active = ((up_hidden + 1.0) * gate_hidden * jax.nn.sigmoid(1.702 * gate_hidden)).astype(jnp.bfloat16)
    return jnp.dot(active, down_full, preferred_element_type=jnp.float32)

def reference(queries, new_kv, cache, lengths, residual, o_proj, router, w_gate, w_up, w_down, routes):
    request_count = residual.shape[1]
    block_count = request_count // REQ_DEV
    gate_full = w_gate.reshape(EXPERTS, SPLIT, D, FFS).transpose(0, 2, 1, 3).reshape(EXPERTS, D, SPLIT * FFS)
    up_full = w_up.reshape(EXPERTS, SPLIT, D, FFS).transpose(0, 2, 1, 3).reshape(EXPERTS, D, SPLIT * FFS)
    down_full = w_down.reshape(EXPERTS, SPLIT * FFS, D)
    attended_list = []
    layer_list = []
    for batch_index in range(MB):
        live_rows = jnp.tile(lengths[batch_index], KVH)
        mixed = attention_rows(queries[batch_index], new_kv[batch_index], cache[batch_index], live_rows)
        heads_all = mixed.reshape(KVH, request_count, QPK * HD).transpose(1, 0, 2).reshape(request_count, KVH * QPK * HD)
        attended = (residual[batch_index].astype(jnp.float32) + jnp.dot(heads_all, o_proj, preferred_element_type=jnp.float32)).astype(jnp.bfloat16)
        attended_wide = attended.astype(jnp.float32)
        normed = (attended_wide * lax.rsqrt(lax.optimization_barrier(jnp.mean(attended_wide * attended_wide, axis=1, keepdims=True)) + 1e-05)).astype(jnp.bfloat16)
        logits = jnp.dot(normed, router, preferred_element_type=jnp.float32)
        route_ids = routes[batch_index]
        chosen = jnp.take_along_axis(logits, route_ids, axis=1)
        gates = 1.0 / lax.optimization_barrier(jnp.sum(jnp.exp(chosen[:, None, :] - chosen[:, :, None]), axis=2))
        one_hot = (route_ids[:, :, None] == jnp.arange(EXPERTS, dtype=jnp.int32)[None, None, :]).astype(jnp.int32)
        by_block = one_hot.reshape(block_count, REQ_DEV * TOPK, EXPERTS)
        earlier = jnp.cumsum(by_block, axis=1) - by_block
        ranks = lax.optimization_barrier(jnp.sum(earlier * by_block, axis=2)).reshape(request_count, TOPK)
        block_of_row = (jnp.arange(request_count, dtype=jnp.int32) // REQ_DEV)[:, None]
        slot_index = (route_ids * (block_count * CAP) + block_of_row * CAP + ranks).astype(jnp.int32)
        buffer = jnp.zeros((EXPERTS * block_count * CAP, D), jnp.bfloat16)
        buffer = buffer.at[slot_index.reshape(-1)].set(jnp.repeat(normed, TOPK, axis=0))
        expert_rows = buffer.reshape(EXPERTS, block_count * CAP, D)
        produced = lax.map(expert_block, (expert_rows, gate_full, up_full, down_full))
        flat_out = produced.reshape(EXPERTS * block_count * CAP, D)
        picked = jnp.take(flat_out, slot_index, axis=0)
        mixture = lax.optimization_barrier(jnp.sum(gates[:, :, None] * picked, axis=1))
        layer = (attended_wide + mixture).astype(jnp.bfloat16)
        attended_list.append(attended)
        layer_list.append(layer)
    return (jnp.stack(attended_list), jnp.stack(layer_list))
```

```python
import functools
import math

import jax
import jax.numpy as jnp
from jax import lax
from jax.experimental import pallas as pl
from jax.experimental.pallas import tpu as pltpu
from jax.sharding import PartitionSpec as P

HD = 64
LANES = 128
EPS = 1e-05
MESH = pl.DeviceIdType.MESH


def flip(value, mask):
    bit = 1
    result = value
    while bit <= mask:
        if mask & bit:
            result = result + bit - 2 * bit * ((value // bit) % 2)
        bit *= 2
    return result


def dot_t(left, right):
    return lax.dot_general(left, right, (((1,), (1,)), ((), ())), preferred_element_type=jnp.float32)


def cuts(total, pieces, unit):
    step = -(-total // (pieces * unit)) * unit
    edges = list(range(0, total, step)) + [total]
    return list(zip(edges[:-1], edges[1:]))


def publish(att_ref, lay_ref, att_out, lay_out):
    att_out[...] = att_ref[...]
    lay_out[...] = lay_ref[...]


def schedule():
    return [
        0, 0, 0, 1, 1, 1, 0, 0, 1, 1, 0, 1, 0, 0, 0, 1, 0, 1, 0, 0, 0, 1, 1, 0,
        1, 0, 1, 1, 0, 0, 1, 0, 0, 1, 0, 0, 1, 1, 0, 1, 1, 1, 1, 0, 0, 1, 0, 1,
        1, 0, 0, 1, 0, 1, 1, 0, 1, 1,
    ]


def layer_kernel(
    cfg,
    q_ref, nk_ref, len_ref, cache_ref, res_ref, o_ref, router_ref, gate_ref, up_ref, down_ref, routes_ref,
    att_ref, lay_ref,
    cache_v, o_v, gate_v, up_v, down_v, query_v, mixed_v, router_v, q_v, nk_v, len_v, res_v, routes_v, att_v, lay_v,
    *more,
):
    n, group, width, subs, per_expert, batches, columns, units = cfg
    more = list(more)

    def take(count):
        return [more.pop(0) for _ in range(count)]

    parts = len(columns)
    heads_v, kept_v, give_y, land_y, give_z, land_z, wide_v, rows_v, xs_v, act_v = (take(batches) for _ in range(10))
    sums_v, give_c2, land_c2, give_y2, land_y2, give_z2, land_z2 = (
        [take(parts) for _ in range(batches)] for _ in range(7)
    )
    cache_sem, load_sem, small_sem, out_sem, swap_sem, red_y_sem, red_z_sem, ag_sem, mix_sem, mix_z_sem = more

    me = lax.axis_index("req")
    depth = res_ref.shape[2]
    own = res_ref.shape[1]
    experts = router_ref.shape[0]
    hidden = gate_ref.shape[0]
    far = n // 4
    mine = me % group
    y_bit = (me // group) % 2
    sources = n // group // 2
    slot = me // group // 2
    z_place = me // 4
    if group < 4:
        local = jnp.where(z_place // 2 == mine, 1, 0)
        last = local * (z_place % 2) + (1 - local) * (1 - mine % 2)
    else:
        last = 1 - mine % 2
    turns = subs // 2
    offs = list(range(far - 1, 0, -1))
    tail = depth // LANES * LANES
    lead = depth - tail

    def cache_copy(m, k):
        return pltpu.make_async_copy(
            cache_ref.at[m, pl.ds(k * 16, 16)], cache_v.at[m, pl.ds(k * 16, 16)], cache_sem.at[m, k]
        )

    def remote(src, dst, sems, device):
        return pltpu.make_async_remote_copy(
            src_ref=src, dst_ref=dst, send_sem=sems[0], recv_sem=sems[1], device_id={"req": device}, device_id_type=MESH
        )

    loads = [
        pltpu.make_async_copy(src, dst, load_sem.at[i])
        for i, (src, dst) in enumerate(
            ((o_ref, o_v.at[mine]), (gate_ref, gate_v), (up_ref, up_v), (down_ref, down_v))
        )
    ]
    early = [
        pltpu.make_async_copy(src, dst, small_sem.at[i])
        for i, (src, dst) in enumerate(((q_ref, q_v), (nk_ref, nk_v), (len_ref, len_v)))
    ]
    later = [
        pltpu.make_async_copy(src, dst, small_sem.at[3 + i])
        for i, (src, dst) in enumerate(
            (
                (res_ref, res_v),
                (routes_ref, routes_v),
                (router_ref, router_v.at[lead : lead + experts]),
                (router_ref, router_v.at[lead + experts : lead + 2 * experts]),
            )
        )
    ]
    barrier = pltpu.get_barrier_semaphore()
    masks = [mask for mask in range(1, n) if group != 2 or not mask & 2 or mask == 2]
    for mask in masks:
        pl.semaphore_signal(barrier, inc=1, device_id={"req": flip(me, mask)}, device_id_type=MESH)
    for copy in early:
        copy.start()
    for k in range(turns):
        cache_copy(0, k).start()
    loads[0].start()
    for copy in later:
        copy.start()
    for m in range(1, batches):
        for k in range(turns):
            cache_copy(m, k).start()
    swaps = []
    for j in range(1, group):
        sems = (swap_sem.at[0, j], swap_sem.at[1, j])
        swaps.append(remote(o_ref, o_v.at[mine], sems, flip(me, j)))

    def enter():
        pl.semaphore_wait(barrier, len(masks))
        for swap in swaps:
            swap.start()
        for load in loads[1:]:
            load.start()

    factor = 1.0 / math.sqrt(HD)
    lane = lax.broadcasted_iota(jnp.int32, (16, LANES), 1)
    position = lax.broadcasted_iota(jnp.int32, (8, LANES), 1)
    first = mine * subs * 8

    def attend(m, k):
        cache_copy(m, k).wait()
        base = k * 16
        here = pl.ds(pl.multiple_of(base, 16), 16)
        fresh = nk_v[m, here, :].astype(jnp.float32)
        fresh = jnp.broadcast_to(fresh[:, None, :], (16, 8, LANES)).reshape(128, LANES)
        for j in range(4):
            pair = q_v[m, here, j * LANES : (j + 1) * LANES].astype(jnp.float32)
            query_v[pl.ds(2 * j, 16, stride=8), :] = jnp.where(lane < HD, pair, 0.0)
            query_v[pl.ds(2 * j + 1, 16, stride=8), :] = jnp.where(lane < HD, pltpu.roll(pair, HD, 1), 0.0)
        masked = []
        for r in range(16):
            score = dot_t(query_v[r * 8 : r * 8 + 8, :].astype(jnp.bfloat16), cache_v[m, base + r])
            live = position < len_v[m, first + base + r]
            masked.append(jnp.where(live, score * factor, -jnp.inf))
        masked = jnp.concatenate(masked, axis=0)
        own_score = jnp.sum(query_v[...] * fresh, axis=1, keepdims=True) * factor
        top = jnp.maximum(jnp.max(masked, axis=1, keepdims=True), own_score)
        weight = jnp.exp(masked - top)
        weight_own = jnp.exp(own_score - top)
        total = jnp.sum(weight, axis=1, keepdims=True) + weight_own
        probs = weight / total
        prob_own = (weight_own / total).astype(jnp.bfloat16).astype(jnp.float32)
        mixed = []
        for r in range(16):
            mixed.append(
                jnp.dot(
                    probs[r * 8 : r * 8 + 8].astype(jnp.bfloat16),
                    cache_v[m, base + r],
                    preferred_element_type=jnp.float32,
                )
            )
        mixed_v[...] = jnp.concatenate(mixed, axis=0) + prob_own * fresh
        head = [mixed_v[pl.ds(h, 16, stride=8), :] for h in range(8)]
        y_at = (k % 2 + y_bit) % 2
        z_at = (k // 2 + last) % 2
        for j in range(4):
            pair = jnp.where(lane < HD, pltpu.roll(head[2 * j], HD, 1), head[2 * j + 1])
            heads_v[m][y_at, z_at, :, j * LANES : (j + 1) * LANES] = pair.astype(jnp.bfloat16)

    def attend_range(m, low, high):
        def body(k, carry):
            attend(m, k)
            return carry

        lax.fori_loop(low, high, body, 0)

    def project(m):
        lhs = heads_v[m][...].reshape(subs * 8, heads_v[m].shape[3])
        half = subs * 4
        for low, high in columns:
            part = 0.0
            for p in range(group):
                part = part + dot_t(lhs[:, p * width : (p + 1) * width], o_v[p, low:high, :])
            kept_v[m][:, :, :, low:high] = part[:half].reshape(2, 2, own, high - low)
            give_y[m][:, :, :, low:high] = part[half:].reshape(2, 2, own, high - low).astype(jnp.bfloat16)

    def reduce_y(m, at):
        sems = (red_y_sem.at[m, 0, at], red_y_sem.at[m, 1, at])
        return remote(give_y[m].at[at], land_y[m].at[at], sems, flip(me, group))

    def reduce_z(m, at, c):
        z_at = (last + at) % 2
        dest = mine * subs + 4 * z_at + 2 * y_bit + c
        sems = (red_z_sem.at[m, 0, at * 2 + c], red_z_sem.at[m, 1, slot])
        return dest, remote(give_z[m].at[at, c], land_z[m].at[slot], sems, dest)

    def reduce_step(m, at):
        reduce_y(m, at).wait_recv()
        for c in range(2):
            value = kept_v[m][at, c] + land_y[m][at, c].astype(jnp.float32)
            give_z[m][at, c] = value.astype(jnp.bfloat16)
            dest, copy = reduce_z(m, at, c)

            @pl.when(dest != me)
            def _():
                copy.start()

            @pl.when(dest == me)
            def _():
                pltpu.make_async_copy(give_z[m].at[at, c], land_z[m].at[slot], red_z_sem.at[m, 1, slot]).start()

    def reduce_end(m):
        value = res_v[m].astype(jnp.float32)
        summed = 0.0
        for s in range(sources):
            pltpu.make_async_copy(land_z[m].at[s], land_z[m].at[s], red_z_sem.at[m, 1, s]).wait()
            summed = summed + land_z[m][s].astype(jnp.float32)
        return (value + summed).astype(jnp.bfloat16)

    def reduce_drain(m):
        for at in range(2):
            reduce_y(m, at).wait_send()
            for c in range(2):
                dest, copy = reduce_z(m, at, c)

                @pl.when(dest != me)
                def _():
                    copy.wait_send()

    def out_copy(m, i):
        src, dst = ((att_v, att_ref), (lay_v, lay_ref))[i]
        return pltpu.make_async_copy(src.at[m], dst.at[m], out_sem.at[m, i])

    def norm_rows(m, value):
        att_v[m] = value
        out_copy(m, 0).start()
        value = value.astype(jnp.float32)
        wide_v[m][...] = value
        square = jnp.sum(value * value, axis=1, keepdims=True)
        normed = value * lax.rsqrt(square / depth + EPS)
        row = normed.astype(jnp.bfloat16)
        logits = dot_t(row, router_v[...])
        ids = lax.broadcasted_iota(jnp.int32, (own, LANES), 1)
        named_ids = jnp.where(ids < lead + experts, ids - lead, ids - lead - experts).astype(jnp.float32)
        r_at = lax.broadcasted_iota(jnp.int32, (own, own), 0)
        c_at = lax.broadcasted_iota(jnp.int32, (own, own), 1)
        pick = jnp.where(r_at == c_at, 1.0, 0.0).astype(jnp.bfloat16)
        routes = dot_t(pick, routes_v[m].astype(jnp.float32).astype(jnp.bfloat16))
        named = jnp.zeros((own, LANES), jnp.float32)
        for t in range(routes_ref.shape[1]):
            named = jnp.where(named_ids == routes[:, t : t + 1], 1.0, named)
        inside = jnp.where(ids < lead + experts, named, 0.0)
        live = jnp.where(named > 0.0, logits, -jnp.inf)
        power = jnp.exp(live - jnp.max(live, axis=1, keepdims=True))
        total = jnp.sum(jnp.where(inside > 0.0, power, 0.0), axis=1, keepdims=True)
        gates = power / total
        high = gates.astype(jnp.bfloat16).astype(jnp.float32)
        gates = jnp.where(ids < lead + experts, high, gates - high)
        end = jnp.concatenate([normed[:, tail:], jnp.zeros((own, LANES - lead), jnp.float32)], axis=1)
        rows_v[m][0, 0, 0, :, :tail] = row[:, :tail]
        rows_v[m][0, 0, 0, :, tail:] = jnp.where(ids < lead, end, gates).astype(jnp.bfloat16)

    def spread_z(m, o):
        sems = (ag_sem.at[m, 0, 0, o], ag_sem.at[m, 1, 0, o])
        return remote(rows_v[m].at[0, 0, 0], rows_v[m].at[0, 0, o], sems, flip(me, 4 * o))

    def spread_y(m, o):
        sems = (ag_sem.at[m, 0, 1, o], ag_sem.at[m, 1, 1, o])
        return remote(rows_v[m].at[0, 0, o], rows_v[m].at[0, 1, o], sems, flip(me, 2))

    def spread_c(m, y, o):
        sems = (ag_sem.at[m, 0, 2 + y, o], ag_sem.at[m, 1, 2 + y, o])
        return remote(rows_v[m].at[0, y, o], rows_v[m].at[1, y, o], sems, flip(me, 1))

    expert = me * units // per_expert
    tiles = n * own // 128
    blocks = 128 // own
    hidden_cuts = cuts(hidden, max(1, hidden // 480), 256)

    def tile_rows(m, tile):
        spans = rows_v[m].shape[:3]
        if tiles == 1:
            return rows_v[m][...]
        per = spans[2] // blocks if spans[2] >= blocks else None
        if per:
            c, rest = divmod(tile, spans[1] * per)
            y, z = divmod(rest, per)
            return rows_v[m][c, y, z * blocks : (z + 1) * blocks]
        c = tile * blocks // (spans[1] * spans[2])
        ys = blocks // spans[2]
        y = tile * blocks // spans[2] % spans[1]
        return rows_v[m][c, y : y + ys]

    def fill(m, tile):
        wide = tile_rows(m, tile).astype(jnp.float32).reshape(128, rows_v[m].shape[4])
        xs_v[m][...] = wide.astype(jnp.bfloat16)

    def expand(m, tile, low, high):
        x = xs_v[m][:, :depth]
        g = dot_t(x, gate_v[low:high, :])
        u = dot_t(x, up_v[low:high, :])
        active = ((u + 1.0) * g * jax.nn.sigmoid(1.702 * g)).astype(jnp.bfloat16)
        act_v[m][tile * 128 : (tile + 1) * 128, low:high] = active

    def gate_of(m, tile):
        wide = tile_rows(m, tile)[..., tail:].astype(jnp.float32).reshape(128, LANES)
        column = lax.broadcasted_iota(jnp.int32, (128, LANES), 1)
        chosen = jnp.where(column == lead + expert, wide, 0.0) + jnp.where(column == lead + experts + expert, wide, 0.0)
        return jnp.sum(chosen, axis=1, keepdims=True)

    def contract(m, q):
        low, high = columns[q]
        half = tiles // 2
        for tile in range(tiles):
            part = jnp.dot(
                act_v[m][tile * 128 : (tile + 1) * 128, :], down_v[:, low:high], preferred_element_type=jnp.float32
            )
            part = part * gate_of(m, tile)
            if tiles == 1:
                sums_v[m][q][...] = part[:64].reshape(sums_v[m][q].shape)
                give_c2[m][q][...] = part[64:].reshape(sums_v[m][q].shape).astype(jnp.bfloat16)
                continue
            span = sums_v[m][q].shape
            per = 128 // own
            at = tile % half * per
            y, z = at // span[1], at % span[1]
            if span[1] >= per:
                where = (y, slice(z, z + per))
                shape = (per, own, high - low)
            else:
                where = (slice(y, y + per // span[1]),)
                shape = (per // span[1], span[1], own, high - low)
            if tile < half:
                sums_v[m][q][where] = part.reshape(shape)
            else:
                give_c2[m][q][where] = part.reshape(shape).astype(jnp.bfloat16)
        mix_c(m, q).start()

    def mix_c(m, q):
        return remote(give_c2[m][q], land_c2[m][q], (mix_sem.at[m, 0, 0, q], mix_sem.at[m, 1, 0, q]), flip(me, 1))

    def mix_y(m, q):
        return remote(give_y2[m][q], land_y2[m][q], (mix_sem.at[m, 0, 1, q], mix_sem.at[m, 1, 1, q]), flip(me, 2))

    def mix_z(m, q, o):
        sems = (mix_z_sem.at[m, 0, q, o], mix_z_sem.at[m, 1, q, o])
        return remote(give_z2[m][q].at[o], land_z2[m][q].at[o], sems, flip(me, 4 * o))

    def mix_step_y(m, q):
        mix_c(m, q).wait_recv()
        give_y2[m][q][...] = (sums_v[m][q][1] + land_c2[m][q][1].astype(jnp.float32)).astype(jnp.bfloat16)
        mix_y(m, q).start()
        sums_v[m][q][0] = sums_v[m][q][0] + land_c2[m][q][0].astype(jnp.float32)

    def mix_step_z(m, q):
        mix_y(m, q).wait_recv()
        for o in offs:
            give_z2[m][q][o] = (sums_v[m][q][0, o] + land_y2[m][q][o].astype(jnp.float32)).astype(jnp.bfloat16)
            mix_z(m, q, o).start()
        sums_v[m][q][0, 0] = sums_v[m][q][0, 0] + land_y2[m][q][0].astype(jnp.float32)

    def mix_end(m, q):
        low, high = columns[q]
        value = sums_v[m][q][0, 0]
        for o in offs[::-1]:
            mix_z(m, q, o).wait_recv()
            value = value + land_z2[m][q][o].astype(jnp.float32)
        lay_v[m, :, low:high] = (wide_v[m][:, low:high] + value).astype(jnp.bfloat16)

    def mix_drain(m):
        for q in range(parts):
            mix_c(m, q).wait_send()
            mix_y(m, q).wait_send()
            for o in offs:
                mix_z(m, q, o).wait_send()

    def chain(m):
        if m == 0:
            for copy in early:
                copy.wait()
            router_v[:lead, :] = jnp.zeros((lead, depth), jnp.bfloat16)
            rest = LANES - lead - 2 * experts
            router_v[lead + 2 * experts :, :] = jnp.zeros((rest, depth), jnp.bfloat16)
            attend_range(m, 0, turns // 4)
            enter()
            attend_range(m, turns // 4, turns // 2)
        else:
            attend_range(m, 0, turns // 2)
        yield "attend"
        attend_range(m, turns // 2, turns)
        yield "attend"
        if m == 0:
            loads[0].wait()
            for copy in later:
                copy.wait()
            for swap in swaps:
                swap.wait()
        project(m)
        reduce_y(m, 1).start()
        reduce_y(m, 0).start()
        yield "project"
        reduce_step(m, 1)
        yield "reduce"
        reduce_step(m, 0)
        yield "reduce"
        norm_rows(m, reduce_end(m))
        for o in offs:
            spread_z(m, o).start()
        spread_y(m, 0).start()
        spread_c(m, 0, 0).start()
        reduce_drain(m)
        yield "norm"
        for o in offs[::-1]:
            spread_z(m, o).wait_recv()
            spread_y(m, o).start()
            spread_c(m, 0, o).start()
            yield "spread_z"
        for o in [0] + offs[::-1]:
            spread_y(m, o).wait_recv()
            spread_c(m, 1, o).start()
            yield "spread_y"
        for y in range(2):
            for o in [0] + offs[::-1]:
                spread_c(m, y, o).wait_recv()
        if m == 0:
            for load in loads[1:]:
                load.wait()
        for tile in range(tiles):
            fill(m, tile)
            for low, high in hidden_cuts:
                expand(m, tile, low, high)
                yield "expand"
        for o in offs:
            spread_z(m, o).wait_send()
        for o in range(far):
            spread_y(m, o).wait_send()
            for y in range(2):
                spread_c(m, y, o).wait_send()
        for q in range(parts):
            contract(m, q)
            yield "contract"
            if q:
                mix_step_y(m, q - 1)
                yield "mix_y"
        mix_step_y(m, parts - 1)
        yield "mix_y"
        for q in range(parts):
            mix_step_z(m, q)
            yield "mix_z"
        for q in range(parts):
            mix_end(m, q)
            yield "end"
        out_copy(m, 1).start()
        mix_drain(m)
        for i in range(2):
            out_copy(m, i).wait()
        yield "drain"

    chains = [chain(m) for m in range(batches)]
    live = [True] * batches
    for m in schedule():
        if live[m] and next(chains[m], None) is None:
            live[m] = False
    turn = 0
    while any(live):
        if live[turn] and next(chains[turn], None) is None:
            live[turn] = False
        turn = (turn + 1) % batches


def shards(queries, new_kv, cache, lengths, residual, o_proj, router, w_gate, w_up, w_down, routes):
    n = lax.axis_size("req")
    batches, local, q_cols = queries.shape
    depth = residual.shape[2]
    own = residual.shape[1]
    width = o_proj.shape[0]
    group = q_cols // width
    subs = local // own
    heads = q_cols // HD
    experts = router.shape[1]
    entries = w_gate.shape[0]
    per_expert = max(1, n * entries // experts)
    hidden = entries * w_gate.shape[2]
    columns = cuts(depth, 3, LANES)
    far = n // 4
    reach = depth // LANES * LANES + LANES
    if depth % LANES + 2 * experts > LANES or subs != 8 or own != 8 or n * own % 128:
        raise ValueError("sizes")

    gate_t = jnp.swapaxes(w_gate, 1, 2).reshape(hidden, depth)
    up_t = jnp.swapaxes(w_up, 1, 2).reshape(hidden, depth)
    down = w_down.reshape(hidden, depth)
    f32, b16 = jnp.float32, jnp.bfloat16
    vmem = pl.BlockSpec(memory_space=pltpu.VMEM)
    hbm = pl.BlockSpec(memory_space=pl.ANY)

    def each(shape, dtype):
        return [pltpu.VMEM(shape, dtype)] * batches

    def pieces(shape, dtype):
        return [pltpu.VMEM(shape + (high - low,), dtype) for low, high in columns] * batches

    scratch = [
        pltpu.VMEM(cache.shape, b16),
        pltpu.VMEM((group, depth, width), b16),
        pltpu.VMEM(gate_t.shape, b16),
        pltpu.VMEM(up_t.shape, b16),
        pltpu.VMEM(down.shape, b16),
        pltpu.VMEM((16 * heads, LANES), f32),
        pltpu.VMEM((16 * heads, LANES), f32),
        pltpu.VMEM((LANES, depth), b16),
        pltpu.VMEM(queries.shape, b16),
        pltpu.VMEM(new_kv.shape, b16),
        pltpu.SMEM(lengths.shape, jnp.int32),
        pltpu.VMEM(residual.shape, b16),
        pltpu.VMEM((batches, routes.shape[2], own), jnp.int32),
        pltpu.VMEM(residual.shape, b16),
        pltpu.VMEM(residual.shape, b16),
        *each((2, 2, 16, q_cols), b16),
        *each((2, 2, own, depth), f32),
        *each((2, 2, own, depth), b16),
        *each((2, 2, own, depth), b16),
        *each((2, 2, own, depth), b16),
        *each((n // group // 2, own, depth), b16),
        *each((own, depth), f32),
        *each((2, 2, far, own, reach), b16),
        *each((128, reach), b16),
        *each((n * own, hidden), b16),
        *pieces((2, far, own), f32),
        *pieces((2, far, own), b16),
        *pieces((2, far, own), b16),
        *pieces((far, own), b16),
        *pieces((far, own), b16),
        *pieces((far, own), b16),
        *pieces((far, own), b16),
        pltpu.SemaphoreType.DMA((batches, subs // 2)),
        pltpu.SemaphoreType.DMA((4,)),
        pltpu.SemaphoreType.DMA((7,)),
        pltpu.SemaphoreType.DMA((batches, 2)),
        pltpu.SemaphoreType.DMA((2, group)),
        pltpu.SemaphoreType.DMA((batches, 2, 2)),
        pltpu.SemaphoreType.DMA((batches, 2, max(4, n // group // 2))),
        pltpu.SemaphoreType.DMA((batches, 2, 4, far)),
        pltpu.SemaphoreType.DMA((batches, 2, 2, len(columns))),
        pltpu.SemaphoreType.DMA((batches, 2, len(columns), far)),
    ]
    out = jax.ShapeDtypeStruct(residual.shape, b16)
    results = pl.pallas_call(
        functools.partial(layer_kernel, (n, group, width, subs, per_expert, batches, columns, entries)),
        out_shape=(out, out),
        in_specs=[hbm] * 11,
        out_specs=(hbm, hbm),
        scratch_shapes=scratch,
        compiler_params=pltpu.CompilerParams(
            collective_id=0, has_side_effects=True, vmem_limit_bytes=67043328
        ),
        name="moe_layer",
    )(
        queries, new_kv, lengths, cache, residual, o_proj.T, router.T, gate_t, up_t, down,
        jnp.swapaxes(routes, 1, 2),
    )
    return pl.pallas_call(
        publish, out_shape=(out, out), in_specs=[vmem, vmem], out_specs=(vmem, vmem), name="publish"
    )(*results)


def solution(mesh):
    placed = (
        P(None, ("groups", "req"), None),
        P(None, ("groups", "req"), None),
        P(None, ("groups", "req"), None, None),
        P(None, "groups"),
        P(None, ("groups", "req"), None),
        P("req", None),
        P(),
        P("req", None, None),
        P("req", None, None),
        P("req", None, None),
        P(None, ("groups", "req"), None),
    )
    if tuple(mesh.axis_names) != ("groups", "req"):
        raise ValueError("mesh axes")
    return jax.shard_map(
        shards,
        mesh=mesh,
        in_specs=placed,
        out_specs=(P(None, ("groups", "req"), None), P(None, ("groups", "req"), None)),
        check_vma=False,
    )
```

```python
import functools
import math

import jax
import jax.numpy as jnp
from jax import lax
from jax.experimental import pallas as pl
from jax.experimental.pallas import tpu as pltpu
from jax.sharding import PartitionSpec as P

HD = 64
LANES = 128
EPS = 1e-05
MESH = pl.DeviceIdType.MESH


def flip(value, mask):
    bit = 1
    result = value
    while bit <= mask:
        if mask & bit:
            result = result + bit - 2 * bit * ((value // bit) % 2)
        bit *= 2
    return result


def dot_t(left, right):
    return lax.dot_general(left, right, (((1,), (1,)), ((), ())), preferred_element_type=jnp.float32)


def cuts(total, pieces, unit):
    step = -(-total // (pieces * unit)) * unit
    edges = list(range(0, total, step)) + [total]
    return list(zip(edges[:-1], edges[1:]))


def publish(att_ref, lay_ref, att_out, lay_out):
    att_out[...] = att_ref[...]
    lay_out[...] = lay_ref[...]


def schedule():
    return [
        0, 0, 0, 1, 1, 1, 0, 0, 1, 2, 1, 2, 2, 0, 2, 2, 1, 0, 2, 0, 0, 0, 0, 2,
        1, 0, 1, 1, 1, 0, 0, 0, 0, 0, 1, 1, 0, 1, 0, 0, 0, 1, 1, 1, 1, 2, 0, 1,
        1, 1, 1, 0, 1, 0, 0, 1, 1, 0, 1, 0, 0, 1, 1, 0, 1, 1,
    ]


def layer_kernel(
    cfg,
    q_ref, nk_ref, len_ref, cache_ref, res_ref, o_ref, router_ref, gate_ref, up_ref, down_ref, routes_ref,
    att_ref, lay_ref,
    cache_v, o_v, stage_v, gate_v, up_v, down_v, query_v, mixed_v, router_v, router_t, q_v, nk_v, len_v, res_v, routes_v, att_v, lay_v,
    *more,
):
    n, group, width, subs, per_expert, batches, columns, units = cfg
    more = list(more)

    def take(count):
        return [more.pop(0) for _ in range(count)]

    parts = len(columns)
    heads_v, kept_v, give_y, land_y, give_z, land_z, wide_v, rows_v, xs_v, act_v = (take(batches) for _ in range(10))
    sums_v, give_c2, land_c2, give_y2, land_y2, give_z2, land_z2 = (
        [take(parts) for _ in range(batches)] for _ in range(7)
    )
    cache_sem, load_sem, stage_sem, small_sem, out_sem, swap_sem, red_y_sem, red_z_sem, ag_sem, mix_sem, mix_z_sem = more

    me = lax.axis_index("req")
    depth = res_ref.shape[2]
    own = res_ref.shape[1]
    experts = router_ref.shape[0]
    hidden = gate_ref.shape[0]
    far = n // 4
    mine = me % group
    y_bit = (me // group) % 2
    sources = n // group // 2
    slot = me // group // 2
    z_place = me // 4
    if group < 4:
        local = jnp.where(z_place // 2 == mine, 1, 0)
        last = local * (z_place % 2) + (1 - local) * (1 - mine % 2)
    else:
        last = 1 - mine % 2
    turns = subs // 2
    offs = list(range(far - 1, 0, -1))
    tail = depth // LANES * LANES
    lead = depth - tail

    def cache_copy(m, k):
        return pltpu.make_async_copy(
            cache_ref.at[m, pl.ds(k * 16, 16)], cache_v.at[m, pl.ds(k * 16, 16)], cache_sem.at[m, k]
        )

    def remote(src, dst, sems, device):
        return pltpu.make_async_remote_copy(
            src_ref=src, dst_ref=dst, send_sem=sems[0], recv_sem=sems[1], device_id={"req": device}, device_id_type=MESH
        )

    loads = [
        pltpu.make_async_copy(src, dst, load_sem.at[i])
        for i, (src, dst) in enumerate(
            ((o_ref, o_v.at[mine]), (down_ref, down_v))
        )
    ]
    spans = list(zip(range(0, hidden, 384), [*range(384, hidden, 384), hidden]))

    def stage_copy(i, k):
        low, high = spans[k]
        src = (gate_ref, up_ref)[i]
        return pltpu.make_async_copy(src.at[low:high], stage_v.at[low:high], stage_sem.at[i, k])
    early = [
        pltpu.make_async_copy(src, dst, small_sem.at[i])
        for i, (src, dst) in enumerate(((q_ref, q_v), (nk_ref, nk_v), (len_ref, len_v)))
    ]
    later = [
        pltpu.make_async_copy(src, dst, small_sem.at[3 + i])
        for i, (src, dst) in enumerate(
            (
                (res_ref, res_v),
                (routes_ref, routes_v),
                (router_ref, router_v.at[lead : lead + experts]),
                (router_ref, router_v.at[lead + experts : lead + 2 * experts]),
            )
        )
    ]
    barrier = pltpu.get_barrier_semaphore()
    masks = [mask for mask in range(1, n) if group != 2 or not mask & 2 or mask == 2]
    for mask in masks:
        pl.semaphore_signal(barrier, inc=1, device_id={"req": flip(me, mask)}, device_id_type=MESH)
    for copy in early:
        copy.start()
    for k in range(turns):
        cache_copy(0, k).start()
    loads[0].start()
    for copy in later:
        copy.start()
    for m in range(1, batches):
        for k in range(turns):
            cache_copy(m, k).start()
    swaps = []
    for j in range(1, group):
        sems = (swap_sem.at[0, j], swap_sem.at[1, j])
        swaps.append(remote(o_ref, o_v.at[mine], sems, flip(me, j)))

    def enter():
        pl.semaphore_wait(barrier, len(masks))
        for swap in swaps:
            swap.start()
        for k in range(len(spans)):
            stage_copy(0, k).start()
        loads[1].start()

    def prepare():
        for i, turned in enumerate((gate_v, up_v)):
            for k, (low, high) in enumerate(spans):
                stage_copy(i, k).wait()
                for start in range(0, depth, 384):
                    stop = min(depth, start + 384)
                    turned[start:stop, low:high] = stage_v[low:high, start:stop].T
                if i == 0:
                    stage_copy(1, k).start()
                yield "prepare"

    factor = 1.0 / math.sqrt(HD)
    lane = lax.broadcasted_iota(jnp.int32, (16, LANES), 1)
    position = lax.broadcasted_iota(jnp.int32, (8, LANES), 1)
    first = mine * subs * 8

    def attend(m, k):
        cache_copy(m, k).wait()
        base = k * 16
        here = pl.ds(pl.multiple_of(base, 16), 16)
        fresh = nk_v[m, here, :].astype(jnp.float32)
        fresh = jnp.broadcast_to(fresh[:, None, :], (16, 8, LANES)).reshape(128, LANES)
        for j in range(4):
            pair = q_v[m, here, j * LANES : (j + 1) * LANES].astype(jnp.float32)
            query_v[pl.ds(2 * j, 16, stride=8), :] = jnp.where(lane < HD, pair, 0.0)
            query_v[pl.ds(2 * j + 1, 16, stride=8), :] = jnp.where(lane < HD, pltpu.roll(pair, HD, 1), 0.0)
        masked = []
        for r in range(16):
            score = dot_t(query_v[r * 8 : r * 8 + 8, :].astype(jnp.bfloat16), cache_v[m, base + r])
            live = position < len_v[m, first + base + r]
            masked.append(jnp.where(live, score * factor, -jnp.inf))
        masked = jnp.concatenate(masked, axis=0)
        own_score = jnp.sum(query_v[...] * fresh, axis=1, keepdims=True) * factor
        top = jnp.maximum(jnp.max(masked, axis=1, keepdims=True), own_score)
        weight = jnp.exp(masked - top)
        weight_own = jnp.exp(own_score - top)
        total = jnp.sum(weight, axis=1, keepdims=True) + weight_own
        probs = weight / total
        prob_own = (weight_own / total).astype(jnp.bfloat16).astype(jnp.float32)
        mixed = []
        for r in range(16):
            mixed.append(
                jnp.dot(
                    probs[r * 8 : r * 8 + 8].astype(jnp.bfloat16),
                    cache_v[m, base + r],
                    preferred_element_type=jnp.float32,
                )
            )
        mixed_v[...] = jnp.concatenate(mixed, axis=0) + prob_own * fresh
        head = [mixed_v[pl.ds(h, 16, stride=8), :] for h in range(8)]
        y_at = (k % 2 + y_bit) % 2
        z_at = (k // 2 + last) % 2
        for j in range(4):
            pair = jnp.where(lane < HD, pltpu.roll(head[2 * j], HD, 1), head[2 * j + 1])
            heads_v[m][y_at, z_at, :, j * LANES : (j + 1) * LANES] = pair.astype(jnp.bfloat16)

    def attend_range(m, low, high):
        def body(k, carry):
            attend(m, k)
            return carry

        lax.fori_loop(low, high, body, 0)

    def project(m):
        lhs = heads_v[m][...].reshape(subs * 8, heads_v[m].shape[3])
        half = subs * 4
        for low, high in columns:
            part = 0.0
            for p in range(group):
                part = part + dot_t(lhs[:, p * width : (p + 1) * width], o_v[p, low:high, :])
            kept_v[m][:, :, :, low:high] = part[:half].reshape(2, 2, own, high - low)
            give_y[m][:, :, :, low:high] = part[half:].reshape(2, 2, own, high - low).astype(jnp.bfloat16)

    def reduce_y(m, at):
        sems = (red_y_sem.at[m, 0, at], red_y_sem.at[m, 1, at])
        return remote(give_y[m].at[at], land_y[m].at[at], sems, flip(me, group))

    def reduce_z(m, at, c):
        z_at = (last + at) % 2
        dest = mine * subs + 4 * z_at + 2 * y_bit + c
        sems = (red_z_sem.at[m, 0, at * 2 + c], red_z_sem.at[m, 1, slot])
        return dest, remote(give_z[m].at[at, c], land_z[m].at[slot], sems, dest)

    def reduce_step(m, at):
        reduce_y(m, at).wait_recv()
        for c in range(2):
            value = kept_v[m][at, c] + land_y[m][at, c].astype(jnp.float32)
            give_z[m][at, c] = value.astype(jnp.bfloat16)
            dest, copy = reduce_z(m, at, c)

            @pl.when(dest != me)
            def _():
                copy.start()

            @pl.when(dest == me)
            def _():
                pltpu.make_async_copy(give_z[m].at[at, c], land_z[m].at[slot], red_z_sem.at[m, 1, slot]).start()

    def reduce_end(m):
        value = res_v[m].astype(jnp.float32)
        summed = 0.0
        for s in range(sources):
            pltpu.make_async_copy(land_z[m].at[s], land_z[m].at[s], red_z_sem.at[m, 1, s]).wait()
            summed = summed + land_z[m][s].astype(jnp.float32)
        return (value + summed).astype(jnp.bfloat16)

    def reduce_drain(m):
        for at in range(2):
            reduce_y(m, at).wait_send()
            for c in range(2):
                dest, copy = reduce_z(m, at, c)

                @pl.when(dest != me)
                def _():
                    copy.wait_send()

    def out_copy(m, i):
        src, dst = ((att_v, att_ref), (lay_v, lay_ref))[i]
        return pltpu.make_async_copy(src.at[m], dst.at[m], out_sem.at[m, i])

    def norm_rows(m, value):
        att_v[m] = value
        out_copy(m, 0).start()
        value = value.astype(jnp.float32)
        wide_v[m][...] = value
        square = jnp.sum(value * value, axis=1, keepdims=True)
        normed = value * lax.rsqrt(square / depth + EPS)
        row = normed.astype(jnp.bfloat16)
        logits = jnp.dot(row, router_t[...], preferred_element_type=jnp.float32)
        ids = lax.broadcasted_iota(jnp.int32, (own, LANES), 1)
        named_ids = jnp.where(ids < lead + experts, ids - lead, ids - lead - experts).astype(jnp.float32)
        r_at = lax.broadcasted_iota(jnp.int32, (own, own), 0)
        c_at = lax.broadcasted_iota(jnp.int32, (own, own), 1)
        pick = jnp.where(r_at == c_at, 1.0, 0.0).astype(jnp.bfloat16)
        routes = dot_t(pick, routes_v[m].astype(jnp.float32).astype(jnp.bfloat16))
        named = jnp.zeros((own, LANES), jnp.float32)
        for t in range(routes_ref.shape[1]):
            named = jnp.where(named_ids == routes[:, t : t + 1], 1.0, named)
        inside = jnp.where(ids < lead + experts, named, 0.0)
        live = jnp.where(named > 0.0, logits, -jnp.inf)
        power = jnp.exp(live - jnp.max(live, axis=1, keepdims=True))
        total = jnp.sum(jnp.where(inside > 0.0, power, 0.0), axis=1, keepdims=True)
        gates = power / total
        high = gates.astype(jnp.bfloat16).astype(jnp.float32)
        gates = jnp.where(ids < lead + experts, high, gates - high)
        end = jnp.concatenate([normed[:, tail:], jnp.zeros((own, LANES - lead), jnp.float32)], axis=1)
        rows_v[m][0, 0, 0, :, :tail] = row[:, :tail]
        rows_v[m][0, 0, 0, :, tail:] = jnp.where(ids < lead, end, gates).astype(jnp.bfloat16)

    def spread_z(m, o):
        sems = (ag_sem.at[m, 0, 0, o], ag_sem.at[m, 1, 0, o])
        return remote(rows_v[m].at[0, 0, 0], rows_v[m].at[0, 0, o], sems, flip(me, 4 * o))

    def spread_y(m, o):
        sems = (ag_sem.at[m, 0, 1, o], ag_sem.at[m, 1, 1, o])
        return remote(rows_v[m].at[0, 0, o], rows_v[m].at[0, 1, o], sems, flip(me, 2))

    def spread_c(m, y, o):
        sems = (ag_sem.at[m, 0, 2 + y, o], ag_sem.at[m, 1, 2 + y, o])
        return remote(rows_v[m].at[0, y, o], rows_v[m].at[1, y, o], sems, flip(me, 1))

    expert = me * units // per_expert
    tiles = n * own // 128
    blocks = 128 // own
    hidden_cuts = cuts(hidden, max(1, hidden // 480), 256)

    def tile_rows(m, tile):
        spans = rows_v[m].shape[:3]
        if tiles == 1:
            return rows_v[m][...]
        per = spans[2] // blocks if spans[2] >= blocks else None
        if per:
            c, rest = divmod(tile, spans[1] * per)
            y, z = divmod(rest, per)
            return rows_v[m][c, y, z * blocks : (z + 1) * blocks]
        c = tile * blocks // (spans[1] * spans[2])
        ys = blocks // spans[2]
        y = tile * blocks // spans[2] % spans[1]
        return rows_v[m][c, y : y + ys]

    def fill(m, tile):
        wide = tile_rows(m, tile).astype(jnp.float32).reshape(128, rows_v[m].shape[4])
        xs_v[m][...] = wide.astype(jnp.bfloat16)

    def expand(m, tile, low, high):
        x = xs_v[m][:, :depth]
        g = jnp.dot(x, gate_v[:, low:high], preferred_element_type=jnp.float32)
        u = jnp.dot(x, up_v[:, low:high], preferred_element_type=jnp.float32)
        active = ((u + 1.0) * g * jax.nn.sigmoid(1.702 * g)).astype(jnp.bfloat16)
        act_v[m][tile * 128 : (tile + 1) * 128, low:high] = active

    def gate_of(m, tile):
        wide = tile_rows(m, tile)[..., tail:].astype(jnp.float32).reshape(128, LANES)
        column = lax.broadcasted_iota(jnp.int32, (128, LANES), 1)
        chosen = jnp.where(column == lead + expert, wide, 0.0) + jnp.where(column == lead + experts + expert, wide, 0.0)
        return jnp.sum(chosen, axis=1, keepdims=True)

    def contract(m, q):
        low, high = columns[q]
        half = tiles // 2
        for tile in range(tiles):
            part = jnp.dot(
                act_v[m][tile * 128 : (tile + 1) * 128, :], down_v[:, low:high], preferred_element_type=jnp.float32
            )
            part = part * gate_of(m, tile)
            if tiles == 1:
                sums_v[m][q][...] = part[:64].reshape(sums_v[m][q].shape)
                give_c2[m][q][...] = part[64:].reshape(sums_v[m][q].shape).astype(jnp.bfloat16)
                continue
            span = sums_v[m][q].shape
            per = 128 // own
            at = tile % half * per
            y, z = at // span[1], at % span[1]
            if span[1] >= per:
                where = (y, slice(z, z + per))
                shape = (per, own, high - low)
            else:
                where = (slice(y, y + per // span[1]),)
                shape = (per // span[1], span[1], own, high - low)
            if tile < half:
                sums_v[m][q][where] = part.reshape(shape)
            else:
                give_c2[m][q][where] = part.reshape(shape).astype(jnp.bfloat16)
        mix_c(m, q).start()

    def mix_c(m, q):
        return remote(give_c2[m][q], land_c2[m][q], (mix_sem.at[m, 0, 0, q], mix_sem.at[m, 1, 0, q]), flip(me, 1))

    def mix_y(m, q):
        return remote(give_y2[m][q], land_y2[m][q], (mix_sem.at[m, 0, 1, q], mix_sem.at[m, 1, 1, q]), flip(me, 2))

    def mix_z(m, q, o):
        sems = (mix_z_sem.at[m, 0, q, o], mix_z_sem.at[m, 1, q, o])
        return remote(give_z2[m][q].at[o], land_z2[m][q].at[o], sems, flip(me, 4 * o))

    def mix_step_y(m, q):
        mix_c(m, q).wait_recv()
        give_y2[m][q][...] = (sums_v[m][q][1] + land_c2[m][q][1].astype(jnp.float32)).astype(jnp.bfloat16)
        mix_y(m, q).start()
        sums_v[m][q][0] = sums_v[m][q][0] + land_c2[m][q][0].astype(jnp.float32)

    def mix_step_z(m, q):
        mix_y(m, q).wait_recv()
        for o in offs:
            give_z2[m][q][o] = (sums_v[m][q][0, o] + land_y2[m][q][o].astype(jnp.float32)).astype(jnp.bfloat16)
            mix_z(m, q, o).start()
        sums_v[m][q][0, 0] = sums_v[m][q][0, 0] + land_y2[m][q][0].astype(jnp.float32)

    def mix_end(m, q):
        low, high = columns[q]
        value = sums_v[m][q][0, 0]
        for o in offs[::-1]:
            mix_z(m, q, o).wait_recv()
            value = value + land_z2[m][q][o].astype(jnp.float32)
        lay_v[m, :, low:high] = (wide_v[m][:, low:high] + value).astype(jnp.bfloat16)

    def mix_drain(m):
        for q in range(parts):
            mix_c(m, q).wait_send()
            mix_y(m, q).wait_send()
            for o in offs:
                mix_z(m, q, o).wait_send()

    def chain(m):
        if m == 0:
            for copy in early:
                copy.wait()
            router_v[:lead, :] = jnp.zeros((lead, depth), jnp.bfloat16)
            rest = LANES - lead - 2 * experts
            router_v[lead + 2 * experts :, :] = jnp.zeros((rest, depth), jnp.bfloat16)
            attend_range(m, 0, turns // 4)
            enter()
            attend_range(m, turns // 4, turns // 2)
        else:
            attend_range(m, 0, turns // 2)
        yield "attend"
        attend_range(m, turns // 2, turns)
        yield "attend"
        if m == 0:
            loads[0].wait()
            for copy in later:
                copy.wait()
            for swap in swaps:
                swap.wait()
        project(m)
        reduce_y(m, 1).start()
        reduce_y(m, 0).start()
        if m == 0:
            router_t[...] = router_v[...].T
        yield "project"
        reduce_step(m, 1)
        yield "reduce"
        reduce_step(m, 0)
        yield "reduce"
        norm_rows(m, reduce_end(m))
        for o in offs:
            spread_z(m, o).start()
        spread_y(m, 0).start()
        spread_c(m, 0, 0).start()
        reduce_drain(m)
        yield "norm"
        for o in offs[::-1]:
            spread_z(m, o).wait_recv()
            spread_y(m, o).start()
            spread_c(m, 0, o).start()
            yield "spread_z"
        for o in [0] + offs[::-1]:
            spread_y(m, o).wait_recv()
            spread_c(m, 1, o).start()
            yield "spread_y"
        for y in range(2):
            for o in [0] + offs[::-1]:
                spread_c(m, y, o).wait_recv()
        for _ in ready:
            pass
        if m == 0:
            loads[1].wait()
        for tile in range(tiles):
            fill(m, tile)
            for low, high in hidden_cuts:
                expand(m, tile, low, high)
                yield "expand"
        for o in offs:
            spread_z(m, o).wait_send()
        for o in range(far):
            spread_y(m, o).wait_send()
            for y in range(2):
                spread_c(m, y, o).wait_send()
        for q in range(parts):
            contract(m, q)
            yield "contract"
            if q:
                mix_step_y(m, q - 1)
                yield "mix_y"
        mix_step_y(m, parts - 1)
        yield "mix_y"
        for q in range(parts):
            mix_step_z(m, q)
            yield "mix_z"
        for q in range(parts):
            mix_end(m, q)
            yield "end"
        out_copy(m, 1).start()
        mix_drain(m)
        for i in range(2):
            out_copy(m, i).wait()
        yield "drain"

    ready = prepare()
    chains = [chain(m) for m in range(batches)]
    live = [True] * batches
    for m in schedule():
        if m == batches:
            next(ready, None)
        elif live[m] and next(chains[m], None) is None:
            live[m] = False
    turn = 0
    while any(live):
        if live[turn] and next(chains[turn], None) is None:
            live[turn] = False
        turn = (turn + 1) % batches


def shards(queries, new_kv, cache, lengths, residual, o_proj, router, w_gate, w_up, w_down, routes):
    n = lax.axis_size("req")
    batches, local, q_cols = queries.shape
    depth = residual.shape[2]
    own = residual.shape[1]
    width = o_proj.shape[0]
    group = q_cols // width
    subs = local // own
    heads = q_cols // HD
    experts = router.shape[1]
    entries = w_gate.shape[0]
    per_expert = max(1, n * entries // experts)
    hidden = entries * w_gate.shape[2]
    columns = cuts(depth, 3, LANES)
    far = n // 4
    reach = depth // LANES * LANES + LANES
    if depth % LANES + 2 * experts > LANES or subs != 8 or own != 8 or n * own % 128:
        raise ValueError("sizes")

    gate_t = jnp.swapaxes(w_gate, 1, 2).reshape(hidden, depth)
    up_t = jnp.swapaxes(w_up, 1, 2).reshape(hidden, depth)
    down = w_down.reshape(hidden, depth)
    f32, b16 = jnp.float32, jnp.bfloat16
    vmem = pl.BlockSpec(memory_space=pltpu.VMEM)
    hbm = pl.BlockSpec(memory_space=pl.ANY)

    def each(shape, dtype):
        return [pltpu.VMEM(shape, dtype)] * batches

    def pieces(shape, dtype):
        return [pltpu.VMEM(shape + (high - low,), dtype) for low, high in columns] * batches

    scratch = [
        pltpu.VMEM(cache.shape, b16),
        pltpu.VMEM((group, depth, width), b16),
        pltpu.VMEM(gate_t.shape, b16),
        pltpu.VMEM(gate_t.shape[::-1], b16),
        pltpu.VMEM(gate_t.shape[::-1], b16),
        pltpu.VMEM(down.shape, b16),
        pltpu.VMEM((16 * heads, LANES), f32),
        pltpu.VMEM((16 * heads, LANES), f32),
        pltpu.VMEM((LANES, depth), b16),
        pltpu.VMEM((depth, LANES), b16),
        pltpu.VMEM(queries.shape, b16),
        pltpu.VMEM(new_kv.shape, b16),
        pltpu.SMEM(lengths.shape, jnp.int32),
        pltpu.VMEM(residual.shape, b16),
        pltpu.VMEM((batches, routes.shape[2], own), jnp.int32),
        pltpu.VMEM(residual.shape, b16),
        pltpu.VMEM(residual.shape, b16),
        *each((2, 2, 16, q_cols), b16),
        *each((2, 2, own, depth), f32),
        *each((2, 2, own, depth), b16),
        *each((2, 2, own, depth), b16),
        *each((2, 2, own, depth), b16),
        *each((n // group // 2, own, depth), b16),
        *each((own, depth), f32),
        *each((2, 2, far, own, reach), b16),
        *each((128, reach), b16),
        *each((n * own, hidden), b16),
        *pieces((2, far, own), f32),
        *pieces((2, far, own), b16),
        *pieces((2, far, own), b16),
        *pieces((far, own), b16),
        *pieces((far, own), b16),
        *pieces((far, own), b16),
        *pieces((far, own), b16),
        pltpu.SemaphoreType.DMA((batches, subs // 2)),
        pltpu.SemaphoreType.DMA((2,)),
        pltpu.SemaphoreType.DMA((2, -(-hidden // 384))),
        pltpu.SemaphoreType.DMA((7,)),
        pltpu.SemaphoreType.DMA((batches, 2)),
        pltpu.SemaphoreType.DMA((2, group)),
        pltpu.SemaphoreType.DMA((batches, 2, 2)),
        pltpu.SemaphoreType.DMA((batches, 2, max(4, n // group // 2))),
        pltpu.SemaphoreType.DMA((batches, 2, 4, far)),
        pltpu.SemaphoreType.DMA((batches, 2, 2, len(columns))),
        pltpu.SemaphoreType.DMA((batches, 2, len(columns), far)),
    ]
    out = jax.ShapeDtypeStruct(residual.shape, b16)
    results = pl.pallas_call(
        functools.partial(layer_kernel, (n, group, width, subs, per_expert, batches, columns, entries)),
        out_shape=(out, out),
        in_specs=[hbm] * 11,
        out_specs=(hbm, hbm),
        scratch_shapes=scratch,
        compiler_params=pltpu.CompilerParams(
            collective_id=0, has_side_effects=True, vmem_limit_bytes=67043328
        ),
        name="moe_layer",
    )(
        queries, new_kv, lengths, cache, residual, o_proj.T, router.T, gate_t, up_t, down,
        jnp.swapaxes(routes, 1, 2),
    )
    return pl.pallas_call(
        publish, out_shape=(out, out), in_specs=[vmem, vmem], out_specs=(vmem, vmem), name="publish"
    )(*results)


def solution(mesh):
    placed = (
        P(None, ("groups", "req"), None),
        P(None, ("groups", "req"), None),
        P(None, ("groups", "req"), None, None),
        P(None, "groups"),
        P(None, ("groups", "req"), None),
        P("req", None),
        P(),
        P("req", None, None),
        P("req", None, None),
        P("req", None, None),
        P(None, ("groups", "req"), None),
    )
    if tuple(mesh.axis_names) != ("groups", "req"):
        raise ValueError("mesh axes")
    return jax.shard_map(
        shards,
        mesh=mesh,
        in_specs=placed,
        out_specs=(P(None, ("groups", "req"), None), P(None, ("groups", "req"), None)),
        check_vma=False,
    )
```

```python
import functools
import math

import jax
import jax.numpy as jnp
from jax import lax
from jax.experimental import pallas as pl
from jax.experimental.pallas import tpu as pltpu
from jax.sharding import PartitionSpec as P

HD = 64
LANES = 128
EPS = 1e-05
MESH = pl.DeviceIdType.MESH


def flip(value, mask):
    bit = 1
    result = value
    while bit <= mask:
        if mask & bit:
            result = result + bit - 2 * bit * ((value // bit) % 2)
        bit *= 2
    return result


def dot_t(left, right):
    return lax.dot_general(left, right, (((1,), (1,)), ((), ())), preferred_element_type=jnp.float32)


def cuts(total, pieces, unit):
    step = -(-total // (pieces * unit)) * unit
    edges = list(range(0, total, step)) + [total]
    return list(zip(edges[:-1], edges[1:]))


def publish(att_ref, lay_ref, att_out, lay_out):
    att_out[...] = att_ref[...]
    lay_out[...] = lay_ref[...]


def schedule():
    return [
        0, 0, 0, 1, 1, 0, 0, 1, 0, 2, 2, 0, 2, 2, 1, 2, 1, 2, 1, 1, 0, 1, 0, 0,
        0, 0, 0, 2, 0, 1, 1, 0, 1, 1, 0, 0, 0, 0, 1, 1, 1, 0, 0, 0, 1, 1, 0, 2,
        1, 1, 0, 1, 1, 1, 1, 0, 1, 0, 0, 1, 1, 1, 0, 0, 0, 0, 1, 1, 1, 1,
    ]


def layer_kernel(
    cfg,
    q_ref, nk_ref, len_ref, cache_ref, res_ref, o_ref, router_ref, gate_ref, up_ref, down_ref, routes_ref,
    att_ref, lay_ref,
    cache_v, o_v, stage_v, gate_v, up_v, down_v, query_v, mixed_v, router_v, router_t, q_v, nk_v, len_v, res_v, routes_v, att_v, lay_v,
    *more,
):
    n, group, width, subs, per_expert, batches, columns, halves, units = cfg
    more = list(more)

    def take(count):
        return [more.pop(0) for _ in range(count)]

    parts = len(columns)
    heads_v, wide_v, rows_v, xs_v, act_v = (take(batches) for _ in range(5))
    kept_v, give_y, land_y, give_z, land_z = ([take(len(halves)) for _ in range(batches)] for _ in range(5))
    sums_v, give_c2, land_c2, give_y2, land_y2, give_z2, land_z2 = (
        [take(parts) for _ in range(batches)] for _ in range(7)
    )
    cache_sem, load_sem, stage_sem, small_sem, out_sem, swap_sem, red_y_sem, red_z_sem, ag_sem, mix_sem, mix_z_sem = more

    me = lax.axis_index("req")
    depth = res_ref.shape[2]
    own = res_ref.shape[1]
    experts = router_ref.shape[0]
    hidden = gate_ref.shape[0]
    far = n // 4
    mine = me % group
    y_bit = (me // group) % 2
    sources = n // group // 2
    slot = me // group // 2
    z_place = me // 4
    if group < 4:
        local = jnp.where(z_place // 2 == mine, 1, 0)
        last = local * (z_place % 2) + (1 - local) * (1 - mine % 2)
    else:
        last = 1 - mine % 2
    turns = subs // 2
    offs = list(range(far - 1, 0, -1))
    if far > 2:
        offs[:2] = offs[1::-1]
    tail = depth // LANES * LANES
    lead = depth - tail

    def cache_copy(m, k):
        return pltpu.make_async_copy(
            cache_ref.at[m, pl.ds(k * 16, 16)], cache_v.at[m, pl.ds(k * 16, 16)], cache_sem.at[m, k]
        )

    def remote(src, dst, sems, device):
        return pltpu.make_async_remote_copy(
            src_ref=src, dst_ref=dst, send_sem=sems[0], recv_sem=sems[1], device_id={"req": device}, device_id_type=MESH
        )

    loads = [
        pltpu.make_async_copy(src, dst, load_sem.at[i])
        for i, (src, dst) in enumerate(
            ((o_ref, o_v.at[mine]), (down_ref, down_v))
        )
    ]
    spans = list(zip(range(0, hidden, 384), [*range(384, hidden, 384), hidden]))

    def stage_copy(i, k):
        low, high = spans[k]
        src = (gate_ref, up_ref)[i]
        return pltpu.make_async_copy(src.at[low:high], stage_v.at[low:high], stage_sem.at[i, k])
    early = [
        pltpu.make_async_copy(src, dst, small_sem.at[i])
        for i, (src, dst) in enumerate(((q_ref, q_v), (nk_ref, nk_v), (len_ref, len_v)))
    ]
    later = [
        pltpu.make_async_copy(src, dst, small_sem.at[3 + i])
        for i, (src, dst) in enumerate(
            (
                (res_ref, res_v),
                (routes_ref, routes_v),
                (router_ref, router_v.at[lead : lead + experts]),
                (router_ref, router_v.at[lead + experts : lead + 2 * experts]),
            )
        )
    ]
    barrier = pltpu.get_barrier_semaphore()
    masks = [mask for mask in range(1, n) if group != 2 or not mask & 2 or mask == 2]
    for mask in masks:
        pl.semaphore_signal(barrier, inc=1, device_id={"req": flip(me, mask)}, device_id_type=MESH)
    for copy in early:
        copy.start()
    for k in range(turns):
        cache_copy(0, k).start()
    loads[0].start()
    for copy in later:
        copy.start()
    for m in range(1, batches):
        for k in range(turns):
            cache_copy(m, k).start()
    swaps = []
    for j in range(1, group):
        sems = (swap_sem.at[0, j], swap_sem.at[1, j])
        swaps.append(remote(o_ref, o_v.at[mine], sems, flip(me, j)))

    def enter():
        pl.semaphore_wait(barrier, len(masks))
        for swap in swaps:
            swap.start()
        for k in range(len(spans)):
            stage_copy(0, k).start()
        loads[1].start()

    def prepare():
        for i, turned in enumerate((gate_v, up_v)):
            for k, (low, high) in enumerate(spans):
                stage_copy(i, k).wait()
                for start in range(0, depth, 384):
                    stop = min(depth, start + 384)
                    turned[start:stop, low:high] = stage_v[low:high, start:stop].T
                if i == 0:
                    stage_copy(1, k).start()
                yield "prepare"

    factor = 1.0 / math.sqrt(HD)
    lane = lax.broadcasted_iota(jnp.int32, (16, LANES), 1)
    position = lax.broadcasted_iota(jnp.int32, (8, LANES), 1)
    first = mine * subs * 8

    def attend(m, k):
        cache_copy(m, k).wait()
        base = k * 16
        here = pl.ds(pl.multiple_of(base, 16), 16)
        fresh = nk_v[m, here, :].astype(jnp.float32)
        fresh = jnp.broadcast_to(fresh[:, None, :], (16, 8, LANES)).reshape(128, LANES)
        for j in range(4):
            pair = q_v[m, here, j * LANES : (j + 1) * LANES].astype(jnp.float32)
            query_v[pl.ds(2 * j, 16, stride=8), :] = jnp.where(lane < HD, pair, 0.0)
            query_v[pl.ds(2 * j + 1, 16, stride=8), :] = jnp.where(lane < HD, pltpu.roll(pair, HD, 1), 0.0)
        masked = []
        for r in range(16):
            score = dot_t(query_v[r * 8 : r * 8 + 8, :].astype(jnp.bfloat16), cache_v[m, base + r])
            live = position < len_v[m, first + base + r]
            masked.append(jnp.where(live, score * factor, -jnp.inf))
        masked = jnp.concatenate(masked, axis=0)
        own_score = jnp.sum(query_v[...] * fresh, axis=1, keepdims=True) * factor
        top = jnp.maximum(jnp.max(masked, axis=1, keepdims=True), own_score)
        weight = jnp.exp(masked - top)
        weight_own = jnp.exp(own_score - top)
        total = jnp.sum(weight, axis=1, keepdims=True) + weight_own
        probs = weight / total
        prob_own = (weight_own / total).astype(jnp.bfloat16).astype(jnp.float32)
        mixed = []
        for r in range(16):
            mixed.append(
                jnp.dot(
                    probs[r * 8 : r * 8 + 8].astype(jnp.bfloat16),
                    cache_v[m, base + r],
                    preferred_element_type=jnp.float32,
                )
            )
        mixed_v[...] = jnp.concatenate(mixed, axis=0) + prob_own * fresh
        head = [mixed_v[pl.ds(h, 16, stride=8), :] for h in range(8)]
        y_at = (k % 2 + y_bit) % 2
        z_at = (k // 2 + last) % 2
        for j in range(4):
            pair = jnp.where(lane < HD, pltpu.roll(head[2 * j], HD, 1), head[2 * j + 1])
            heads_v[m][y_at, z_at, :, j * LANES : (j + 1) * LANES] = pair.astype(jnp.bfloat16)

    def attend_range(m, low, high):
        def body(k, carry):
            attend(m, k)
            return carry

        lax.fori_loop(low, high, body, 0)

    def project(m):
        lhs = heads_v[m][...].reshape(subs * 8, heads_v[m].shape[3])
        half = subs * 4
        for h, (low, high) in enumerate(halves):
            part = 0.0
            for p in range(group):
                part = part + dot_t(lhs[:, p * width : (p + 1) * width], o_v[p, low:high, :])
            kept_v[m][h][...] = part[:half].reshape(2, 2, own, high - low)
            give_y[m][h][...] = part[half:].reshape(2, 2, own, high - low).astype(jnp.bfloat16)
            for at in (1, 0):
                reduce_y(m, at, h).start()

    def reduce_y(m, at, h):
        sems = (red_y_sem.at[m, 0, h, at], red_y_sem.at[m, 1, h, at])
        return remote(give_y[m][h].at[at], land_y[m][h].at[at], sems, flip(me, group))

    def reduce_z(m, at, c, h):
        z_at = (last + at) % 2
        dest = mine * subs + 4 * z_at + 2 * y_bit + c
        sems = (red_z_sem.at[m, 0, h, at * 2 + c], red_z_sem.at[m, 1, h, slot])
        return dest, remote(give_z[m][h].at[at, c], land_z[m][h].at[slot], sems, dest)

    def reduce_step(m, at, h):
        reduce_y(m, at, h).wait_recv()
        for c in range(2):
            value = kept_v[m][h][at, c] + land_y[m][h][at, c].astype(jnp.float32)
            give_z[m][h][at, c] = value.astype(jnp.bfloat16)
            dest, copy = reduce_z(m, at, c, h)

            @pl.when(dest != me)
            def _():
                copy.start()

            @pl.when(dest == me)
            def _():
                near = land_z[m][h].at[slot]
                pltpu.make_async_copy(give_z[m][h].at[at, c], near, red_z_sem.at[m, 1, h, slot]).start()

    def reduce_end(m):
        found = []
        for h, (low, high) in enumerate(halves):
            summed = 0.0
            for s in range(sources):
                pltpu.make_async_copy(land_z[m][h].at[s], land_z[m][h].at[s], red_z_sem.at[m, 1, h, s]).wait()
                summed = summed + land_z[m][h][s].astype(jnp.float32)
            found.append((res_v[m, :, low:high].astype(jnp.float32) + summed).astype(jnp.bfloat16))
        return jnp.concatenate(found, axis=1)

    def reduce_drain(m):
        for h in range(len(halves)):
            for at in range(2):
                reduce_y(m, at, h).wait_send()
                for c in range(2):
                    dest, copy = reduce_z(m, at, c, h)

                    @pl.when(dest != me)
                    def _():
                        copy.wait_send()

    def out_copy(m, i):
        src, dst = ((att_v, att_ref), (lay_v, lay_ref))[i]
        return pltpu.make_async_copy(src.at[m], dst.at[m], out_sem.at[m, i])

    def norm_rows(m, value):
        att_v[m] = value
        out_copy(m, 0).start()
        value = value.astype(jnp.float32)
        wide_v[m][...] = value
        square = jnp.sum(value * value, axis=1, keepdims=True)
        normed = value * lax.rsqrt(square / depth + EPS)
        row = normed.astype(jnp.bfloat16)
        logits = jnp.dot(row, router_t[...], preferred_element_type=jnp.float32)
        ids = lax.broadcasted_iota(jnp.int32, (own, LANES), 1)
        named_ids = jnp.where(ids < lead + experts, ids - lead, ids - lead - experts).astype(jnp.float32)
        r_at = lax.broadcasted_iota(jnp.int32, (own, own), 0)
        c_at = lax.broadcasted_iota(jnp.int32, (own, own), 1)
        pick = jnp.where(r_at == c_at, 1.0, 0.0).astype(jnp.bfloat16)
        routes = dot_t(pick, routes_v[m].astype(jnp.float32).astype(jnp.bfloat16))
        named = jnp.zeros((own, LANES), jnp.float32)
        for t in range(routes_ref.shape[1]):
            named = jnp.where(named_ids == routes[:, t : t + 1], 1.0, named)
        inside = jnp.where(ids < lead + experts, named, 0.0)
        live = jnp.where(named > 0.0, logits, -jnp.inf)
        power = jnp.exp(live - jnp.max(live, axis=1, keepdims=True))
        total = jnp.sum(jnp.where(inside > 0.0, power, 0.0), axis=1, keepdims=True)
        gates = power / total
        high = gates.astype(jnp.bfloat16).astype(jnp.float32)
        gates = jnp.where(ids < lead + experts, high, gates - high)
        end = jnp.concatenate([normed[:, tail:], jnp.zeros((own, LANES - lead), jnp.float32)], axis=1)
        rows_v[m][0, 0, 0, :, :tail] = row[:, :tail]
        rows_v[m][0, 0, 0, :, tail:] = jnp.where(ids < lead, end, gates).astype(jnp.bfloat16)

    def spread_z(m, o):
        sems = (ag_sem.at[m, 0, 0, o], ag_sem.at[m, 1, 0, o])
        return remote(rows_v[m].at[0, 0, 0], rows_v[m].at[0, 0, o], sems, flip(me, 4 * o))

    def spread_y(m, o):
        sems = (ag_sem.at[m, 0, 1, o], ag_sem.at[m, 1, 1, o])
        return remote(rows_v[m].at[0, 0, o], rows_v[m].at[0, 1, o], sems, flip(me, 2))

    def spread_c(m, y, o):
        sems = (ag_sem.at[m, 0, 2 + y, o], ag_sem.at[m, 1, 2 + y, o])
        return remote(rows_v[m].at[0, y, o], rows_v[m].at[1, y, o], sems, flip(me, 1))

    expert = me * units // per_expert
    tiles = n * own // 128
    blocks = 128 // own
    hidden_cuts = cuts(hidden, max(1, hidden // 480), 256)

    def tile_rows(m, tile):
        spans = rows_v[m].shape[:3]
        if tiles == 1:
            return rows_v[m][...]
        per = spans[2] // blocks if spans[2] >= blocks else None
        if per:
            c, rest = divmod(tile, spans[1] * per)
            y, z = divmod(rest, per)
            return rows_v[m][c, y, z * blocks : (z + 1) * blocks]
        c = tile * blocks // (spans[1] * spans[2])
        ys = blocks // spans[2]
        y = tile * blocks // spans[2] % spans[1]
        return rows_v[m][c, y : y + ys]

    def fill(m, tile):
        wide = tile_rows(m, tile).astype(jnp.float32).reshape(128, rows_v[m].shape[4])
        xs_v[m][...] = wide.astype(jnp.bfloat16)

    def expand(m, tile, low, high):
        x = xs_v[m][:, :depth]
        g = jnp.dot(x, gate_v[:, low:high], preferred_element_type=jnp.float32)
        u = jnp.dot(x, up_v[:, low:high], preferred_element_type=jnp.float32)
        active = ((u + 1.0) * g * jax.nn.sigmoid(1.702 * g)).astype(jnp.bfloat16)
        act_v[m][tile * 128 : (tile + 1) * 128, low:high] = active

    def gate_of(m, tile):
        wide = tile_rows(m, tile)[..., tail:].astype(jnp.float32).reshape(128, LANES)
        column = lax.broadcasted_iota(jnp.int32, (128, LANES), 1)
        chosen = jnp.where(column == lead + expert, wide, 0.0) + jnp.where(column == lead + experts + expert, wide, 0.0)
        return jnp.sum(chosen, axis=1, keepdims=True)

    def contract(m, q):
        low, high = columns[q]
        half = tiles // 2
        for tile in range(tiles):
            part = jnp.dot(
                act_v[m][tile * 128 : (tile + 1) * 128, :], down_v[:, low:high], preferred_element_type=jnp.float32
            )
            part = part * gate_of(m, tile)
            if tiles == 1:
                sums_v[m][q][...] = part[:64].reshape(sums_v[m][q].shape)
                give_c2[m][q][...] = part[64:].reshape(sums_v[m][q].shape).astype(jnp.bfloat16)
                continue
            span = sums_v[m][q].shape
            per = 128 // own
            at = tile % half * per
            y, z = at // span[1], at % span[1]
            if span[1] >= per:
                where = (y, slice(z, z + per))
                shape = (per, own, high - low)
            else:
                where = (slice(y, y + per // span[1]),)
                shape = (per // span[1], span[1], own, high - low)
            if tile < half:
                sums_v[m][q][where] = part.reshape(shape)
            else:
                give_c2[m][q][where] = part.reshape(shape).astype(jnp.bfloat16)
        mix_c(m, q).start()

    def mix_c(m, q):
        return remote(give_c2[m][q], land_c2[m][q], (mix_sem.at[m, 0, 0, q], mix_sem.at[m, 1, 0, q]), flip(me, 1))

    def mix_y(m, q):
        return remote(give_y2[m][q], land_y2[m][q], (mix_sem.at[m, 0, 1, q], mix_sem.at[m, 1, 1, q]), flip(me, 2))

    def mix_z(m, q, o):
        sems = (mix_z_sem.at[m, 0, q, o], mix_z_sem.at[m, 1, q, o])
        return remote(give_z2[m][q].at[o], land_z2[m][q].at[o], sems, flip(me, 4 * o))

    def mix_step_y(m, q):
        mix_c(m, q).wait_recv()
        give_y2[m][q][...] = (sums_v[m][q][1] + land_c2[m][q][1].astype(jnp.float32)).astype(jnp.bfloat16)
        mix_y(m, q).start()
        sums_v[m][q][0] = sums_v[m][q][0] + land_c2[m][q][0].astype(jnp.float32)

    def mix_step_z(m, q):
        mix_y(m, q).wait_recv()
        for o in offs:
            give_z2[m][q][o] = (sums_v[m][q][0, o] + land_y2[m][q][o].astype(jnp.float32)).astype(jnp.bfloat16)
            mix_z(m, q, o).start()
        sums_v[m][q][0, 0] = sums_v[m][q][0, 0] + land_y2[m][q][0].astype(jnp.float32)

    def mix_end(m, q):
        low, high = columns[q]
        value = sums_v[m][q][0, 0]
        for o in offs[::-1]:
            mix_z(m, q, o).wait_recv()
            value = value + land_z2[m][q][o].astype(jnp.float32)
        lay_v[m, :, low:high] = (wide_v[m][:, low:high] + value).astype(jnp.bfloat16)

    def mix_drain(m):
        for q in range(parts):
            mix_c(m, q).wait_send()
            mix_y(m, q).wait_send()
            for o in offs:
                mix_z(m, q, o).wait_send()

    def chain(m):
        if m == 0:
            for copy in early:
                copy.wait()
            router_v[:lead, :] = jnp.zeros((lead, depth), jnp.bfloat16)
            rest = LANES - lead - 2 * experts
            router_v[lead + 2 * experts :, :] = jnp.zeros((rest, depth), jnp.bfloat16)
            attend_range(m, 0, turns // 4)
            enter()
            attend_range(m, turns // 4, turns // 2)
        else:
            attend_range(m, 0, turns // 2)
        yield "attend"
        attend_range(m, turns // 2, turns)
        yield "attend"
        if m == 0:
            loads[0].wait()
            for copy in later:
                copy.wait()
            for swap in swaps:
                swap.wait()
        project(m)
        if m == 0:
            router_t[...] = router_v[...].T
        yield "project"
        for h in range(len(halves)):
            for at in (1, 0):
                reduce_step(m, at, h)
                yield "reduce"
        norm_rows(m, reduce_end(m))
        for o in offs:
            spread_z(m, o).start()
        spread_y(m, 0).start()
        spread_c(m, 0, 0).start()
        reduce_drain(m)
        yield "norm"
        for o in offs[::-1]:
            spread_z(m, o).wait_recv()
            spread_y(m, o).start()
            spread_c(m, 0, o).start()
            yield "spread_z"
        for o in [0] + offs[::-1]:
            spread_y(m, o).wait_recv()
            spread_c(m, 1, o).start()
            yield "spread_y"
        for y in range(2):
            for o in [0] + offs[::-1]:
                spread_c(m, y, o).wait_recv()
        for _ in ready:
            pass
        if m == 0:
            loads[1].wait()
        for tile in range(tiles):
            fill(m, tile)
            for low, high in hidden_cuts:
                expand(m, tile, low, high)
                yield "expand"
        for o in offs:
            spread_z(m, o).wait_send()
        for o in range(far):
            spread_y(m, o).wait_send()
            for y in range(2):
                spread_c(m, y, o).wait_send()
        for q in range(parts):
            contract(m, q)
            yield "contract"
            if q:
                mix_step_y(m, q - 1)
                yield "mix_y"
        mix_step_y(m, parts - 1)
        yield "mix_y"
        for q in range(parts):
            mix_step_z(m, q)
            yield "mix_z"
        for q in range(parts):
            mix_end(m, q)
            yield "end"
        out_copy(m, 1).start()
        mix_drain(m)
        for i in range(2):
            out_copy(m, i).wait()
        yield "drain"

    ready = prepare()
    chains = [chain(m) for m in range(batches)]
    live = [True] * batches
    for m in schedule():
        if m == batches:
            next(ready, None)
        elif live[m] and next(chains[m], None) is None:
            live[m] = False
    turn = 0
    while any(live):
        if live[turn] and next(chains[turn], None) is None:
            live[turn] = False
        turn = (turn + 1) % batches


def shards(queries, new_kv, cache, lengths, residual, o_proj, router, w_gate, w_up, w_down, routes):
    n = lax.axis_size("req")
    batches, local, q_cols = queries.shape
    depth = residual.shape[2]
    own = residual.shape[1]
    width = o_proj.shape[0]
    group = q_cols // width
    subs = local // own
    heads = q_cols // HD
    experts = router.shape[1]
    entries = w_gate.shape[0]
    per_expert = max(1, n * entries // experts)
    hidden = entries * w_gate.shape[2]
    columns, halves = cuts(depth, 3, LANES), cuts(depth, 2, LANES)
    far = n // 4
    reach = depth // LANES * LANES + LANES
    if depth % LANES + 2 * experts > LANES or subs != 8 or own != 8 or n * own % 128:
        raise ValueError("sizes")

    gate_t = jnp.swapaxes(w_gate, 1, 2).reshape(hidden, depth)
    up_t = jnp.swapaxes(w_up, 1, 2).reshape(hidden, depth)
    down = w_down.reshape(hidden, depth)
    f32, b16 = jnp.float32, jnp.bfloat16
    vmem = pl.BlockSpec(memory_space=pltpu.VMEM)
    hbm = pl.BlockSpec(memory_space=pl.ANY)

    def each(shape, dtype):
        return [pltpu.VMEM(shape, dtype)] * batches

    def pieces(shape, dtype, spans=columns):
        return [pltpu.VMEM(shape + (high - low,), dtype) for low, high in spans] * batches

    scratch = [
        pltpu.VMEM(cache.shape, b16),
        pltpu.VMEM((group, depth, width), b16),
        pltpu.VMEM(gate_t.shape, b16),
        pltpu.VMEM(gate_t.shape[::-1], b16),
        pltpu.VMEM(gate_t.shape[::-1], b16),
        pltpu.VMEM(down.shape, b16),
        pltpu.VMEM((16 * heads, LANES), f32),
        pltpu.VMEM((16 * heads, LANES), f32),
        pltpu.VMEM((LANES, depth), b16),
        pltpu.VMEM((depth, LANES), b16),
        pltpu.VMEM(queries.shape, b16),
        pltpu.VMEM(new_kv.shape, b16),
        pltpu.SMEM(lengths.shape, jnp.int32),
        pltpu.VMEM(residual.shape, b16),
        pltpu.VMEM((batches, routes.shape[2], own), jnp.int32),
        pltpu.VMEM(residual.shape, b16),
        pltpu.VMEM(residual.shape, b16),
        *each((2, 2, 16, q_cols), b16),
        *each((own, depth), f32),
        *each((2, 2, far, own, reach), b16),
        *each((128, reach), b16),
        *each((n * own, hidden), b16),
        *pieces((2, 2, own), f32, halves),
        *pieces((2, 2, own), b16, halves),
        *pieces((2, 2, own), b16, halves),
        *pieces((2, 2, own), b16, halves),
        *pieces((n // group // 2, own), b16, halves),
        *pieces((2, far, own), f32),
        *pieces((2, far, own), b16),
        *pieces((2, far, own), b16),
        *pieces((far, own), b16),
        *pieces((far, own), b16),
        *pieces((far, own), b16),
        *pieces((far, own), b16),
        pltpu.SemaphoreType.DMA((batches, subs // 2)),
        pltpu.SemaphoreType.DMA((2,)),
        pltpu.SemaphoreType.DMA((2, -(-hidden // 384))),
        pltpu.SemaphoreType.DMA((7,)),
        pltpu.SemaphoreType.DMA((batches, 2)),
        pltpu.SemaphoreType.DMA((2, group)),
        pltpu.SemaphoreType.DMA((batches, 2, len(halves), 2)),
        pltpu.SemaphoreType.DMA((batches, 2, len(halves), max(4, n // group // 2))),
        pltpu.SemaphoreType.DMA((batches, 2, 4, far)),
        pltpu.SemaphoreType.DMA((batches, 2, 2, len(columns))),
        pltpu.SemaphoreType.DMA((batches, 2, len(columns), far)),
    ]
    out = jax.ShapeDtypeStruct(residual.shape, b16)
    results = pl.pallas_call(
        functools.partial(layer_kernel, (n, group, width, subs, per_expert, batches, columns, halves, entries)),
        out_shape=(out, out),
        in_specs=[hbm] * 11,
        out_specs=(hbm, hbm),
        scratch_shapes=scratch,
        compiler_params=pltpu.CompilerParams(
            collective_id=0, has_side_effects=True, vmem_limit_bytes=67043328
        ),
        name="moe_layer",
    )(
        queries, new_kv, lengths, cache, residual, o_proj.T, router.T, gate_t, up_t, down,
        jnp.swapaxes(routes, 1, 2),
    )
    return pl.pallas_call(
        publish, out_shape=(out, out), in_specs=[vmem, vmem], out_specs=(vmem, vmem), name="publish"
    )(*results)


def solution(mesh):
    placed = (
        P(None, ("groups", "req"), None),
        P(None, ("groups", "req"), None),
        P(None, ("groups", "req"), None, None),
        P(None, "groups"),
        P(None, ("groups", "req"), None),
        P("req", None),
        P(),
        P("req", None, None),
        P("req", None, None),
        P("req", None, None),
        P(None, ("groups", "req"), None),
    )
    if tuple(mesh.axis_names) != ("groups", "req"):
        raise ValueError("mesh axes")
    return jax.shard_map(
        shards,
        mesh=mesh,
        in_specs=placed,
        out_specs=(P(None, ("groups", "req"), None), P(None, ("groups", "req"), None)),
        check_vma=False,
    )
```
